32 devices in a mesh: dom: 4 (over z), row: 4 (over y, x), col: 2 (over core).
Axes of the slice: x: 2, y: 2, z: 4, core: 2. Of those that a mesh axis runs over, the one named last changes fastest.
Arguments:
- currents: bfloat16 [4, 64, 4096], P('dom', None, ('col', 'row')), may hold values from -6 to 6
- shared_basis: bfloat16 [4, 64, 4096], P('dom', None, 'col'), may hold values from -0.25 to 0.25
- self_v: bfloat16 [4, 8, 8, 64, 512], P('dom', 'row', 'col'), may hold values from -0.25 to 0.25
- self_u: bfloat16 [4, 8, 8, 64, 512], P('dom', 'row', 'col'), may hold values from -0.25 to 0.25
- self_rank: int32 [4, 8, 8], P('dom', 'row', 'col'), may hold values from 16 to 64
- coupling_u: bfloat16 [4, 8, 4, 4, 64, 512], P('dom', 'row', None, 'col'), may hold values from -0.1875 to 0.1875
- coupling_rank: int32 [4, 8, 4, 4], P('dom', 'row', None, 'col'), may hold values from 16 to 64
- link_tiles: int32 [4, 8, 4, 4], P('dom', 'row', None, 'col'), may hold values from 0 to 3
- incident: float32 [4, 64, 4096], P('dom', 'col', 'row'), may hold values from -6 to 6
Outputs:
- residual: float32 [4, 64, 4096], P('dom', 'col', 'row')
The draws below stay inside these ranges and needn't reach their ends.
Inputs may be any that keep to these rules, and one draw needn't show every extreme that they name: `link_tiles`: entries may repeat within a list.
All inputs are finite; a program needn't handle non-finite values.
Results may differ from the reference program's by a relative error of at most 0.0022.
Values may be sent and summed in bfloat16 or wider, within the bound.
A program may use at most 64 MiB of HBM per device.

```python
import jax
import jax.numpy as jnp
from jax import lax

TILE = 512
RANK = 64
ANG = 64
LINKS = 2
PARTS_SIZE = 4
TCB = 4
ROWS = 8
COLS = 8
LINKTOT = 4


def place_ends(result, rng, least, largest):
    longest = result.shape.index(max(result.shape))
    spots = []
    for shift in (0, 1):
        where = [jax.random.randint(jax.random.fold_in(rng, axis), (), 0, length) for axis, length in enumerate(result.shape)]
        where[longest] = (where[longest] + shift) % result.shape[longest]
        spots.append(tuple(where))
    return result.at[spots[0]].set(least).at[spots[1]].set(largest)


def block_levels(key, extent, cuts, least, high):
    def one(dim, parts):
        draws = jax.random.uniform(jax.random.fold_in(jax.random.fold_in(key, 6), dim), (parts,), jnp.float32, least / len(cuts), high / len(cuts))
        return jnp.repeat(jnp.exp(draws), extent[dim] // parts).reshape((-1,) + (1,) * (len(extent) - dim - 1))

    level = one(*cuts[0])
    for cut in cuts[1:]:
        level = level * one(*cut)
    return level


def normal_values(own_key, extent, width, most, pieces=(), kind=jnp.bfloat16):
    values = jax.random.normal(own_key, extent, jnp.float32) * width
    if len(pieces) > 0:
        values = block_levels(own_key, extent, pieces, -0.22, 0.18) * values
    return jnp.clip(values, min=-most, max=most).astype(kind)


def setup_inputs(seed: int = 0) -> dict:
    seeds = jax.random.split(jax.random.key(seed), 10)
    return {
        "currents": normal_values(seeds[0], (PARTS_SIZE, ANG, COLS * TILE), 1.0, 6.0, ((0, 4), (2, 8))),
        "shared_basis": normal_values(seeds[1], (PARTS_SIZE, RANK, COLS * TILE), TILE ** -0.5, 0.25, ((0, 4), (2, 2))),
        "self_v": normal_values(seeds[2], (PARTS_SIZE, ROWS, COLS, RANK, TILE), TILE ** -0.5, 0.25, ((0, 4), (1, 4), (2, 2))),
        "self_u": normal_values(seeds[3], (PARTS_SIZE, ROWS, COLS, RANK, TILE), (COLS * RANK) ** -0.5, 0.25, ((0, 4), (1, 4), (2, 2))),
        "self_rank": place_ends(jax.random.randint(seeds[4], (PARTS_SIZE, ROWS, COLS), RANK // 4, RANK + 1), jax.random.fold_in(seeds[4], 1), RANK // 4, RANK).astype(jnp.int32),
        "coupling_u": normal_values(seeds[5], (PARTS_SIZE, ROWS, PARTS_SIZE, LINKTOT, RANK, TILE), (PARTS_SIZE * LINKTOT * RANK) ** -0.5, 0.1875, ((0, 4), (1, 4), (3, 2))),
        "coupling_rank": place_ends(jax.random.randint(seeds[6], (PARTS_SIZE, ROWS, PARTS_SIZE, LINKTOT), RANK // 4, RANK + 1), jax.random.fold_in(seeds[6], 1), RANK // 4, RANK).astype(jnp.int32),
        "link_tiles": place_ends(jax.random.randint(seeds[7], (PARTS_SIZE, ROWS, PARTS_SIZE, LINKTOT), 0, TCB), jax.random.fold_in(seeds[7], 1), 0, TCB - 1).astype(jnp.int32),
        "incident": normal_values(seeds[8], (PARTS_SIZE, ANG, ROWS * TILE), 1.0, 6.0, ((0, 4), (1, 2), (2, 4)), jnp.float32),
    }


def reference(currents, shared_basis, self_v, self_u, self_rank, coupling_u, coupling_rank, link_tiles, incident):
    levels = jnp.arange(RANK, dtype=jnp.int32)
    current_all = currents.astype(jnp.float32).reshape(PARTS_SIZE, ANG, COLS, TILE)
    bases = shared_basis.astype(jnp.float32).reshape(PARTS_SIZE, RANK, COLS, TILE)
    basisproj = jnp.einsum("ekjn,eajn->ejka", bases, current_all).astype(jnp.bfloat16)
    flat_proj = basisproj.reshape(PARTS_SIZE * COLS, RANK, ANG)
    block_base = (jnp.arange(LINKTOT, dtype=jnp.int32) // LINKS) * TCB
    part_base = jnp.arange(PARTS_SIZE, dtype=jnp.int32)[:, None] * COLS

    def one_part(part_index):
        current_part = lax.dynamic_index_in_dim(current_all, part_index, 0, keepdims=False)
        v_part = lax.dynamic_index_in_dim(self_v, part_index, 0, keepdims=False).astype(jnp.float32)
        u_part = lax.dynamic_index_in_dim(self_u, part_index, 0, keepdims=False).astype(jnp.float32)
        rank_part = lax.dynamic_index_in_dim(self_rank, part_index, 0, keepdims=False)
        keep_self = (levels[None, None, :] < rank_part[:, :, None]).astype(jnp.float32)
        selfproj = jnp.einsum("ijkn,ajn->ijka", v_part, current_part)
        selfproj = (selfproj * keep_self[..., None]).astype(jnp.bfloat16)
        field_self = jnp.einsum("ijkn,ijka->ain", u_part, selfproj.astype(jnp.float32))
        links_part = lax.dynamic_index_in_dim(link_tiles, part_index, 0, keepdims=False)
        picks = (part_base + block_base[None, :])[None, :, :] + links_part
        chosen = jnp.take(flat_proj, picks.reshape(-1).astype(jnp.int32), axis=0)
        chosen = chosen.reshape(ROWS, PARTS_SIZE, LINKTOT, RANK, ANG)
        crank_part = lax.dynamic_index_in_dim(coupling_rank, part_index, 0, keepdims=False)
        keep_cpl = (levels < crank_part[..., None]).astype(jnp.bfloat16)
        chosen = chosen * keep_cpl[..., None]
        cu_part = lax.dynamic_index_in_dim(coupling_u, part_index, 0, keepdims=False).astype(jnp.float32)
        field_cpl = jnp.einsum("iemkn,iemka->ain", cu_part, chosen.astype(jnp.float32))
        field = (field_self + field_cpl).reshape(ANG, ROWS * TILE)
        rhs_part = lax.dynamic_index_in_dim(incident, part_index, 0, keepdims=False)
        return rhs_part - field

    return lax.map(one_part, jnp.arange(PARTS_SIZE, dtype=jnp.int32))
```

```python
import functools

import jax
import jax.numpy as jnp
from jax import lax
from jax.experimental import pallas as pl
from jax.experimental.pallas import tpu as pltpu
from jax.sharding import PartitionSpec as P

MESH = pl.DeviceIdType.MESH
LANES = 128
NT = (((1,), (1,)), ((), ()))


def kernel(
    sizes,
    self_rank,
    coupling_rank,
    link_tiles,
    currents,
    basis,
    self_v,
    self_u,
    coupling_u,
    out,
    cur_all,
    basis_own,
    v_buf,
    u_buf,
    cu_buf,
    proj,
    acc,
    part,
    landed,
    in_sem,
    cur_send,
    cur_recv,
    dom_send,
    dom_recv,
    row_send,
    row_recv,
    col_send,
    col_recv,
):
    doms, rows, cols = sizes
    dom, row, col = (lax.axis_index(name) for name in ("dom", "row", "col"))
    angles = currents.shape[1]
    width = currents.shape[2]
    window, tiles, rank, tile_len = self_v.shape[1:]
    links = coupling_u.shape[3]
    own_tiles = width // tile_len
    fold = max(1, LANES // rank)
    piece = angles // fold
    share = angles // cols

    def dom_at(k):
        return lax.rem(dom + k, doms)

    def row_at(k):
        return lax.rem(row + k, rows)

    def col_at(k):
        return lax.rem(col + k, cols)

    own_columns = pl.ds(pl.multiple_of(row * width, width), width)
    loads = [
        pltpu.make_async_copy(currents.at[0], cur_all.at[row], in_sem.at[0]),
        pltpu.make_async_copy(basis.at[0, :, own_columns], basis_own, in_sem.at[1]),
        pltpu.make_async_copy(self_v.at[0], v_buf, in_sem.at[2]),
        pltpu.make_async_copy(self_u.at[0], u_buf, in_sem.at[3]),
        pltpu.make_async_copy(coupling_u.at[0], cu_buf, in_sem.at[4]),
    ]
    for load in loads:
        load.start()

    barrier = pltpu.get_barrier_semaphore()
    for k in range(1, doms):
        pl.semaphore_signal(barrier, inc=1, device_id=(dom_at(k), row, col), device_id_type=MESH)
    for k in range(1, rows):
        pl.semaphore_signal(barrier, inc=1, device_id=(dom, row_at(k), col), device_id_type=MESH)
    for k in range(1, cols):
        pl.semaphore_signal(barrier, inc=1, device_id=(dom, row, col_at(k)), device_id_type=MESH)

    loads[0].wait()
    loads[1].wait()
    for o in range(own_tiles):
        span = slice(o * tile_len, (o + 1) * tile_len)
        own = lax.dot_general(
            cur_all[row, :, span], basis_own[:, span], NT, preferred_element_type=jnp.float32
        )
        folded = jnp.concatenate([own[f * piece : (f + 1) * piece] for f in range(fold)], axis=1)
        proj[dom, row, o] = folded.astype(jnp.bfloat16)

    pl.semaphore_wait(barrier, doms + rows + cols - 3)

    to_dom = [
        pltpu.make_async_remote_copy(
            src_ref=proj.at[dom, row],
            dst_ref=proj.at[dom, row],
            send_sem=dom_send.at[k - 1],
            recv_sem=dom_recv.at[k - 1],
            device_id=(dom_at(k), row, col),
            device_id_type=MESH,
        )
        for k in range(1, doms)
    ]
    for copy in to_dom:
        copy.start()

    def forward(source, slot):
        copies = [
            pltpu.make_async_remote_copy(
                src_ref=proj.at[source, row],
                dst_ref=proj.at[source, row],
                send_sem=row_send.at[slot, k - 1],
                recv_sem=row_recv.at[slot, k - 1],
                device_id=(dom, row_at(k), col),
                device_id_type=MESH,
            )
            for k in range(1, rows)
        ]
        for copy in copies:
            copy.start()
        return copies

    to_row = forward(dom, 0)
    spread = [
        pltpu.make_async_remote_copy(
            src_ref=cur_all.at[row],
            dst_ref=cur_all.at[row],
            send_sem=cur_send.at[k - 1],
            recv_sem=cur_recv.at[k - 1],
            device_id=(dom, row_at(k), col),
            device_id_type=MESH,
        )
        for k in range(1, rows)
    ]
    for copy in spread:
        copy.start()

    for k in range(1, doms):
        to_dom[k - 1].wait_recv()
        to_row += forward(dom_at(doms - k), k)

    lane = lax.broadcasted_iota(jnp.int32, (angles, rank), 1)
    for load in loads[2:]:
        load.wait()
    for copy in spread:
        copy.wait_recv()
    kept = [[] for _ in range(window)]
    for j in range(tiles):
        o = j % own_tiles
        cur = cur_all[j // own_tiles, :, o * tile_len : (o + 1) * tile_len]
        for t in range(window):
            level = lax.dot_general(cur, v_buf[t, j], NT, preferred_element_type=jnp.float32)
            kept[t].append(jnp.where(lane < self_rank[0, t, j], level, 0.0))
    for t in range(window):
        left = jnp.concatenate(kept[t], axis=1).astype(jnp.bfloat16)
        acc[t] = jnp.dot(
            left, u_buf[t].reshape(tiles * rank, tile_len), preferred_element_type=jnp.float32
        )

    for copy in to_row:
        copy.wait_recv()
    pick_lane = lax.broadcasted_iota(jnp.int32, (piece, rank), 1)
    to_col = []
    for t in range(window):
        lefts = [[] for _ in range(fold)]
        for e in range(doms):
            for m in range(links):
                tile = link_tiles[0, t, m, e]
                held = proj[e, tile // own_tiles, tile % own_tiles] if own_tiles > 1 else proj[e, tile, 0]
                held = held.astype(jnp.float32)
                keep = pick_lane < coupling_rank[0, t, m, e]
                for f in range(fold):
                    lefts[f].append(jnp.where(keep, held[:, f * rank : (f + 1) * rank], 0.0))
        left = jnp.concatenate([jnp.concatenate(one, axis=1) for one in lefts], axis=0)
        part[t] = acc[t] + jnp.dot(
            left.astype(jnp.bfloat16),
            cu_buf[t].reshape(doms * links * rank, tile_len),
            preferred_element_type=jnp.float32,
        )
        for k in range(1, cols):
            theirs = pl.ds(pl.multiple_of(col_at(k) * share, share), share)
            copy = pltpu.make_async_remote_copy(
                src_ref=part.at[t, theirs],
                dst_ref=landed.at[k - 1, t],
                send_sem=col_send.at[k - 1, t],
                recv_sem=col_recv.at[k - 1, t],
                device_id=(dom, row, col_at(k)),
                device_id_type=MESH,
            )
            copy.start()
            to_col.append(copy)

    for copy in to_dom + to_row + spread:
        copy.wait_send()
    mine = pl.ds(pl.multiple_of(col * share, share), share)
    for t in range(window):
        total = part[t, mine]
        for k in range(1, cols):
            to_col[t * (cols - 1) + k - 1].wait_recv()
            total = total + landed[k - 1, t]
        out[:, t * tile_len : (t + 1) * tile_len] = total
    for copy in to_col:
        copy.wait_send()


def shards(
    currents,
    shared_basis,
    self_v,
    self_u,
    self_rank,
    coupling_u,
    coupling_rank,
    link_tiles,
    incident,
):
    doms, rows, cols = (lax.axis_size(name) for name in ("dom", "row", "col"))
    angles, width = currents.shape[1:]
    window, tiles, rank, tile_len = self_v.shape[1:]
    links = coupling_u.shape[3]
    own_tiles = width // tile_len
    fold = max(1, LANES // rank)
    share = angles // cols
    bf16, f32 = jnp.bfloat16, jnp.float32
    dma = pltpu.SemaphoreType.DMA
    smem = pl.BlockSpec(memory_space=pltpu.SMEM)
    stay = pl.BlockSpec(memory_space=pl.ANY)
    summed = pl.pallas_call(
        functools.partial(kernel, (doms, rows, cols)),
        out_shape=jax.ShapeDtypeStruct((share, window * tile_len), f32),
        in_specs=[smem] * 3 + [stay] * 5,
        out_specs=pl.BlockSpec(memory_space=pltpu.VMEM),
        scratch_shapes=[
            pltpu.VMEM((rows, angles, width), bf16),
            pltpu.VMEM((rank, width), bf16),
            pltpu.VMEM((window, tiles, rank, tile_len), bf16),
            pltpu.VMEM((window, tiles, rank, tile_len), bf16),
            pltpu.VMEM((window, doms, links, rank, tile_len), bf16),
            pltpu.VMEM((doms, rows, own_tiles, angles // fold, fold * rank), bf16),
            pltpu.VMEM((window, angles, tile_len), f32),
            pltpu.VMEM((window, angles, tile_len), f32),
            pltpu.VMEM((cols - 1, window, share, tile_len), f32),
            dma((5,)),
            dma((rows - 1,)),
            dma((rows - 1,)),
            dma((doms - 1,)),
            dma((doms - 1,)),
            dma((doms, rows - 1)),
            dma((doms, rows - 1)),
            dma((cols - 1, window)),
            dma((cols - 1, window)),
        ],
        compiler_params=pltpu.CompilerParams(collective_id=0, has_side_effects=True),
    )(self_rank, jnp.swapaxes(coupling_rank, 2, 3), jnp.swapaxes(link_tiles, 2, 3), currents, shared_basis, self_v, self_u, coupling_u)
    return (incident[0] - summed)[None]


def solution(mesh):
    return jax.shard_map(
        shards,
        mesh=mesh,
        in_specs=(
            P("dom", None, ("col", "row")),
            P("dom", None, "col"),
            P("dom", "row", "col", None, None),
            P("dom", "row", "col", None, None),
            P("dom", "row", "col"),
            P("dom", "row", None, "col", None, None),
            P("dom", "row", None, "col"),
            P("dom", "row", None, "col"),
            P("dom", "col", "row"),
        ),
        out_specs=P("dom", "col", "row"),
        check_vma=False,
    )
```

```python
import functools

import jax
import jax.numpy as jnp
from jax import lax
from jax.experimental import pallas as pl
from jax.experimental.pallas import tpu as pltpu
from jax.sharding import PartitionSpec as P

MESH = pl.DeviceIdType.MESH
LANES = 128
NT = (((1,), (1,)), ((), ()))


def kernel(
    sizes,
    self_rank_in,
    coupling_rank_in,
    link_tiles_in,
    currents,
    basis,
    self_v,
    self_u,
    coupling_u,
    out,
    self_rank,
    coupling_rank,
    link_tiles,
    cur_all,
    basis_own,
    v_buf,
    u_buf,
    cu_buf,
    proj,
    acc,
    part,
    landed,
    in_sem,
    cur_send,
    cur_recv,
    dom_send,
    dom_recv,
    row_send,
    row_recv,
    col_send,
    col_recv,
):
    doms, rows, cols = sizes
    dom, row, col = (lax.axis_index(name) for name in ("dom", "row", "col"))
    angles = currents.shape[1]
    width = currents.shape[2]
    window, tiles, rank, tile_len = self_v.shape[1:]
    links = coupling_u.shape[3]
    own_tiles = width // tile_len
    fold = max(1, LANES // rank)
    piece = angles // fold
    share = angles // cols

    def dom_at(k):
        return lax.rem(dom + k, doms)

    def row_at(k):
        return lax.rem(row + k, rows)

    def col_at(k):
        return lax.rem(col + k, cols)

    own_columns = pl.ds(pl.multiple_of(row * width, width), width)
    loads = [
        pltpu.make_async_copy(currents.at[0], cur_all.at[row], in_sem.at[0]),
        pltpu.make_async_copy(basis.at[0, :, own_columns], basis_own, in_sem.at[1]),
        pltpu.make_async_copy(self_v.at[0], v_buf, in_sem.at[2]),
        pltpu.make_async_copy(self_u.at[0], u_buf, in_sem.at[3]),
        pltpu.make_async_copy(coupling_u.at[0], cu_buf, in_sem.at[4]),
        pltpu.make_async_copy(self_rank_in, self_rank, in_sem.at[5]),
        pltpu.make_async_copy(coupling_rank_in, coupling_rank, in_sem.at[6]),
        pltpu.make_async_copy(link_tiles_in, link_tiles, in_sem.at[7]),
    ]
    for load in loads:
        load.start()

    barrier = pltpu.get_barrier_semaphore()
    for k in range(1, doms):
        pl.semaphore_signal(barrier, inc=1, device_id=(dom_at(k), row, col), device_id_type=MESH)
    for k in range(1, rows):
        pl.semaphore_signal(barrier, inc=1, device_id=(dom, row_at(k), col), device_id_type=MESH)
    for k in range(1, cols):
        pl.semaphore_signal(barrier, inc=1, device_id=(dom, row, col_at(k)), device_id_type=MESH)

    loads[0].wait()
    loads[1].wait()
    for o in range(own_tiles):
        span = slice(o * tile_len, (o + 1) * tile_len)
        own = lax.dot_general(
            cur_all[row, :, span], basis_own[:, span], NT, preferred_element_type=jnp.float32
        )
        folded = jnp.concatenate([own[f * piece : (f + 1) * piece] for f in range(fold)], axis=1)
        proj[dom, row, o] = folded.astype(jnp.bfloat16)

    pl.semaphore_wait(barrier, doms + rows + cols - 3)

    to_dom = [
        pltpu.make_async_remote_copy(
            src_ref=proj.at[dom, row],
            dst_ref=proj.at[dom, row],
            send_sem=dom_send.at[k - 1],
            recv_sem=dom_recv.at[k - 1],
            device_id=(dom_at(k), row, col),
            device_id_type=MESH,
        )
        for k in range(1, doms)
    ]
    for copy in to_dom:
        copy.start()

    def forward(source, slot):
        copies = [
            pltpu.make_async_remote_copy(
                src_ref=proj.at[source, row],
                dst_ref=proj.at[source, row],
                send_sem=row_send.at[slot, k - 1],
                recv_sem=row_recv.at[slot, k - 1],
                device_id=(dom, row_at(k), col),
                device_id_type=MESH,
            )
            for k in range(1, rows)
        ]
        for copy in copies:
            copy.start()
        return copies

    to_row = forward(dom, 0)
    spread = [
        pltpu.make_async_remote_copy(
            src_ref=cur_all.at[row],
            dst_ref=cur_all.at[row],
            send_sem=cur_send.at[k - 1],
            recv_sem=cur_recv.at[k - 1],
            device_id=(dom, row_at(k), col),
            device_id_type=MESH,
        )
        for k in range(1, rows)
    ]
    for copy in spread:
        copy.start()

    for k in range(1, doms):
        to_dom[k - 1].wait_recv()
        to_row += forward(dom_at(doms - k), k)

    lane = lax.broadcasted_iota(jnp.int32, (angles, rank), 1)
    for load in loads[2:]:
        load.wait()
    for copy in spread:
        copy.wait_recv()
    kept = [[] for _ in range(window)]
    for j in range(tiles):
        o = j % own_tiles
        cur = cur_all[j // own_tiles, :, o * tile_len : (o + 1) * tile_len]
        for t in range(window):
            level = lax.dot_general(cur, v_buf[t, j], NT, preferred_element_type=jnp.float32)
            kept[t].append(jnp.where(lane < self_rank[0, t, j], level, 0.0))
    for t in range(window):
        left = jnp.concatenate(kept[t], axis=1).astype(jnp.bfloat16)
        acc[t] = jnp.dot(
            left, u_buf[t].reshape(tiles * rank, tile_len), preferred_element_type=jnp.float32
        )

    for copy in to_row:
        copy.wait_recv()
    pick_lane = lax.broadcasted_iota(jnp.int32, (piece, rank), 1)
    to_col = []
    for t in range(window):
        lefts = [[] for _ in range(fold)]
        for e in range(doms):
            for m in range(links):
                tile = link_tiles[0, t, m, e]
                held = proj[e, tile // own_tiles, tile % own_tiles] if own_tiles > 1 else proj[e, tile, 0]
                held = held.astype(jnp.float32)
                keep = pick_lane < coupling_rank[0, t, m, e]
                for f in range(fold):
                    lefts[f].append(jnp.where(keep, held[:, f * rank : (f + 1) * rank], 0.0))
        left = jnp.concatenate([jnp.concatenate(one, axis=1) for one in lefts], axis=0)
        part[t] = acc[t] + jnp.dot(
            left.astype(jnp.bfloat16),
            cu_buf[t].reshape(doms * links * rank, tile_len),
            preferred_element_type=jnp.float32,
        )
        for k in range(1, cols):
            theirs = pl.ds(pl.multiple_of(col_at(k) * share, share), share)
            copy = pltpu.make_async_remote_copy(
                src_ref=part.at[t, theirs],
                dst_ref=landed.at[k - 1, t],
                send_sem=col_send.at[k - 1, t],
                recv_sem=col_recv.at[k - 1, t],
                device_id=(dom, row, col_at(k)),
                device_id_type=MESH,
            )
            copy.start()
            to_col.append(copy)

    for copy in to_dom + to_row + spread:
        copy.wait_send()
    mine = pl.ds(pl.multiple_of(col * share, share), share)
    for t in range(window):
        total = part[t, mine]
        for k in range(1, cols):
            to_col[t * (cols - 1) + k - 1].wait_recv()
            total = total + landed[k - 1, t]
        out[:, t * tile_len : (t + 1) * tile_len] = total
    for copy in to_col:
        copy.wait_send()


def shards(
    currents,
    shared_basis,
    self_v,
    self_u,
    self_rank,
    coupling_u,
    coupling_rank,
    link_tiles,
    incident,
):
    doms, rows, cols = (lax.axis_size(name) for name in ("dom", "row", "col"))
    angles, width = currents.shape[1:]
    window, tiles, rank, tile_len = self_v.shape[1:]
    links = coupling_u.shape[3]
    own_tiles = width // tile_len
    fold = max(1, LANES // rank)
    share = angles // cols
    bf16, f32 = jnp.bfloat16, jnp.float32
    dma = pltpu.SemaphoreType.DMA
    stay = pl.BlockSpec(memory_space=pltpu.HBM)
    ranks, picks = (jnp.swapaxes(x, 2, 3) for x in (coupling_rank, link_tiles))
    summed = pl.pallas_call(
        functools.partial(kernel, (doms, rows, cols)),
        out_shape=jax.ShapeDtypeStruct((share, window * tile_len), f32),
        in_specs=[stay] * 8,
        out_specs=pl.BlockSpec(memory_space=pltpu.VMEM),
        scratch_shapes=[
            pltpu.SMEM(self_rank.shape, jnp.int32),
            pltpu.SMEM(ranks.shape, jnp.int32),
            pltpu.SMEM(picks.shape, jnp.int32),
            pltpu.VMEM((rows, angles, width), bf16),
            pltpu.VMEM((rank, width), bf16),
            pltpu.VMEM((window, tiles, rank, tile_len), bf16),
            pltpu.VMEM((window, tiles, rank, tile_len), bf16),
            pltpu.VMEM((window, doms, links, rank, tile_len), bf16),
            pltpu.VMEM((doms, rows, own_tiles, angles // fold, fold * rank), bf16),
            pltpu.VMEM((window, angles, tile_len), f32),
            pltpu.VMEM((window, angles, tile_len), f32),
            pltpu.VMEM((cols - 1, window, share, tile_len), f32),
            dma((8,)),
            dma((rows - 1,)),
            dma((rows - 1,)),
            dma((doms - 1,)),
            dma((doms - 1,)),
            dma((doms, rows - 1)),
            dma((doms, rows - 1)),
            dma((cols - 1, window)),
            dma((cols - 1, window)),
        ],
        compiler_params=pltpu.CompilerParams(collective_id=0, has_side_effects=True, vmem_limit_bytes=16 << 20),
    )(*(pltpu.with_memory_space_constraint(x, pltpu.HBM) for x in (self_rank, ranks, picks, currents, shared_basis, self_v, self_u, coupling_u)))
    return (incident[0] - summed)[None]


def solution(mesh):
    return jax.shard_map(
        shards,
        mesh=mesh,
        in_specs=(
            P("dom", None, ("col", "row")),
            P("dom", None, "col"),
            P("dom", "row", "col", None, None),
            P("dom", "row", "col", None, None),
            P("dom", "row", "col"),
            P("dom", "row", None, "col", None, None),
            P("dom", "row", None, "col"),
            P("dom", "row", None, "col"),
            P("dom", "col", "row"),
        ),
        out_specs=P("dom", "col", "row"),
        check_vma=False,
    )
```

```python
import functools

import jax
import jax.numpy as jnp
from jax import lax
from jax.experimental import pallas as pl
from jax.experimental.pallas import tpu as pltpu
from jax.sharding import PartitionSpec as P

MESH = pl.DeviceIdType.MESH
LANES = 128
NT = (((1,), (1,)), ((), ()))


def kernel(
    sizes,
    self_rank_in,
    coupling_rank_in,
    link_tiles_in,
    currents,
    basis,
    self_v,
    self_u,
    coupling_u,
    out,
    self_rank,
    coupling_rank,
    link_tiles,
    cur_all,
    basis_own,
    v_buf,
    u_buf,
    cu_buf,
    proj,
    acc,
    part,
    landed,
    in_sem,
    cur_send,
    cur_recv,
    dom_send,
    dom_recv,
    row_send,
    row_recv,
    col_send,
    col_recv,
    straight_send,
    above,
    *hold,
):
    doms, rows, cols = sizes
    dom, row, col = (lax.axis_index(name) for name in ("dom", "row", "col"))
    angles = currents.shape[1]
    width = currents.shape[2]
    window, tiles, rank, tile_len = self_v.shape[1:]
    links = coupling_u.shape[3]
    own_tiles = width // tile_len
    fold = max(1, LANES // rank)
    piece = angles // fold
    share = angles // cols

    def dom_at(k):
        return lax.rem(dom + k, doms)

    def row_at(k):
        return lax.rem(row + k, rows)

    def col_at(k):
        return lax.rem(col + k, cols)

    own_columns = pl.ds(pl.multiple_of(row * width, width), width)
    loads = [
        pltpu.make_async_copy(currents.at[0], cur_all.at[row], in_sem.at[0]),
        pltpu.make_async_copy(basis.at[0, :, own_columns], basis_own, in_sem.at[1]),
        pltpu.make_async_copy(self_v.at[0], v_buf, in_sem.at[2]),
        pltpu.make_async_copy(self_u.at[0], u_buf, in_sem.at[3]),
        pltpu.make_async_copy(coupling_u.at[0], cu_buf, in_sem.at[4]),
        pltpu.make_async_copy(self_rank_in, self_rank, in_sem.at[5]),
        pltpu.make_async_copy(coupling_rank_in, coupling_rank, in_sem.at[6]),
        pltpu.make_async_copy(link_tiles_in, link_tiles, in_sem.at[7]),
    ]
    for load in loads:
        load.start()

    barrier = pltpu.get_barrier_semaphore()
    for k in range(1, doms):

        @pl.when(dom + k < doms)
        def _():
            for b in range(rows):
                pl.semaphore_signal(barrier, inc=1, device_id=(dom_at(k), row_at(b), col), device_id_type=MESH)

    for k in range(1, rows):
        pl.semaphore_signal(barrier, inc=1, device_id=(dom, row_at(k), col), device_id_type=MESH)
    for k in range(1, cols):
        pl.semaphore_signal(barrier, inc=1, device_id=(dom, row, col_at(k)), device_id_type=MESH)
    pl.semaphore_wait(barrier, dom * rows + rows + cols - 2)
    for k in range(1, doms):

        @pl.when(dom + k >= doms)
        def _():
            pl.semaphore_signal(above, inc=1, device_id=(dom_at(k), row, col), device_id_type=MESH)

    loads[0].wait()
    spread = [
        pltpu.make_async_remote_copy(
            src_ref=cur_all.at[row],
            dst_ref=cur_all.at[row],
            send_sem=cur_send.at[k - 1],
            recv_sem=cur_recv.at[k - 1],
            device_id=(dom, row_at(k), col),
            device_id_type=MESH,
        )
        for k in range(1, rows)
    ]
    for copy in spread:
        copy.start()

    loads[1].wait()
    for o in range(own_tiles):
        span = slice(o * tile_len, (o + 1) * tile_len)
        own = lax.dot_general(
            cur_all[row, :, span], basis_own[:, span], NT, preferred_element_type=jnp.float32
        )
        folded = jnp.concatenate([own[f * piece : (f + 1) * piece] for f in range(fold)], axis=1)
        proj[dom, row, o] = folded.astype(jnp.bfloat16)

    to_dom = [
        pltpu.make_async_remote_copy(
            src_ref=proj.at[dom, row],
            dst_ref=proj.at[dom, row],
            send_sem=dom_send.at[k],
            recv_sem=dom_recv.at[k],
            device_id=(dom_at(k), row, col),
            device_id_type=MESH,
        )
        for k in range(1, doms)
    ]
    straight = [
        [
            pltpu.make_async_remote_copy(
                src_ref=proj.at[dom, row],
                dst_ref=proj.at[dom, row],
                send_sem=straight_send.at[k, b - 1],
                recv_sem=row_recv.at[k, b - 1],
                device_id=(dom_at(k), row_at(b), col),
                device_id_type=MESH,
            )
            for b in range(1, rows)
        ]
        for k in range(1, doms)
    ]
    for k in range(1, doms):

        @pl.when(dom + k >= doms)
        def _():
            to_dom[k - 1].start()
            for copy in straight[k - 1]:
                copy.start()

    def forward(source, slot):
        copies = [
            pltpu.make_async_remote_copy(
                src_ref=proj.at[source, row],
                dst_ref=proj.at[source, row],
                send_sem=row_send.at[slot, k - 1],
                recv_sem=row_recv.at[slot, k - 1],
                device_id=(dom, row_at(k), col),
                device_id_type=MESH,
            )
            for k in range(1, rows)
        ]

        @pl.when(slot <= dom)
        def _():
            for copy in copies:
                copy.start()

        return copies

    to_row = [forward(dom, 0)]

    @pl.when(dom + 1 < doms)
    def _():
        pl.semaphore_wait(above, doms - 1 - dom)

    for k in range(1, doms):

        @pl.when(dom + k < doms)
        def _():
            to_dom[k - 1].start()

    lower = 1 - (2 * dom) // doms
    steps = [0] + [i + (doms - 2 * i) * lower for i in range(1, doms)]
    sources = [dom] + [dom_at(doms - k) for k in steps[1:]]
    for k, source in zip(steps[1:], sources[1:]):
        pltpu.make_async_remote_copy(
            src_ref=proj.at[source, row],
            dst_ref=proj.at[source, row],
            send_sem=dom_send.at[k],
            recv_sem=dom_recv.at[k],
            device_id=(source, row, col),
            device_id_type=MESH,
        ).wait_recv()
        to_row.append(forward(source, k))

    lane = lax.broadcasted_iota(jnp.int32, (angles, rank), 1)
    for load in loads[2:]:
        load.wait()
    for copy in spread:
        copy.wait_recv()
    kept = [[] for _ in range(window)]
    for j in range(tiles):
        o = j % own_tiles
        cur = cur_all[j // own_tiles, :, o * tile_len : (o + 1) * tile_len]
        for t in range(window):
            level = lax.dot_general(cur, v_buf[t, j], NT, preferred_element_type=jnp.float32)
            kept[t].append(jnp.where(lane < self_rank[0, t, j], level, 0.0))
    for t in range(window):
        left = jnp.concatenate(kept[t], axis=1).astype(jnp.bfloat16)
        acc[t] = jnp.dot(
            left, u_buf[t].reshape(tiles * rank, tile_len), preferred_element_type=jnp.float32
        )

    pick_lane = lax.broadcasted_iota(jnp.int32, (piece, rank), 1)

    def coupled(t, e, held_all):
        lefts = [[] for _ in range(fold)]
        for m in range(links):
            tile = link_tiles[0, t, m, e]
            held = held_all[tile].astype(jnp.float32)
            keep = pick_lane < coupling_rank[0, t, m, e]
            for f in range(fold):
                lefts[f].append(jnp.where(keep, held[:, f * rank : (f + 1) * rank], 0.0))
        left = jnp.concatenate([jnp.concatenate(one, axis=1) for one in lefts], axis=0)
        return jnp.dot(
            left.astype(jnp.bfloat16),
            cu_buf[t, e].reshape(links * rank, tile_len),
            preferred_element_type=jnp.float32,
        )

    to_col = []
    for i, e in enumerate(sources):
        for copy in to_row[i]:
            copy.wait_recv()
        held_all = hold[i]
        for r in range(rows):
            for o in range(own_tiles):
                held_all[r * own_tiles + o] = proj[e, r, o]
        if i < doms - 1:
            for t in range(window):
                acc[t] += coupled(t, e, held_all)
            continue
        for t in range(window):
            part[t] = acc[t] + coupled(t, e, held_all)
            for k in range(1, cols):
                theirs = pl.ds(pl.multiple_of(col_at(k) * share, share), share)
                copy = pltpu.make_async_remote_copy(
                    src_ref=part.at[t, theirs],
                    dst_ref=landed.at[k - 1, t],
                    send_sem=col_send.at[k - 1, t],
                    recv_sem=col_recv.at[k - 1, t],
                    device_id=(dom, row, col_at(k)),
                    device_id_type=MESH,
                )
                copy.start()
                to_col.append(copy)

    for copy in to_dom + to_row[0] + spread:
        copy.wait_send()
    for k in range(1, doms):

        @pl.when(dom + k >= doms)
        def _():
            for copy in straight[k - 1]:
                copy.wait_send()

    for k, copies in zip(steps[1:], to_row[1:]):

        @pl.when(k <= dom)
        def _():
            for copy in copies:
                copy.wait_send()

    mine = pl.ds(pl.multiple_of(col * share, share), share)
    for t in range(window):
        total = part[t, mine]
        for k in range(1, cols):
            to_col[t * (cols - 1) + k - 1].wait_recv()
            total = total + landed[k - 1, t]
        out[:, t * tile_len : (t + 1) * tile_len] = total
    for copy in to_col:
        copy.wait_send()


def shards(
    currents,
    shared_basis,
    self_v,
    self_u,
    self_rank,
    coupling_u,
    coupling_rank,
    link_tiles,
    incident,
):
    doms, rows, cols = (lax.axis_size(name) for name in ("dom", "row", "col"))
    angles, width = currents.shape[1:]
    window, tiles, rank, tile_len = self_v.shape[1:]
    links = coupling_u.shape[3]
    own_tiles = width // tile_len
    fold = max(1, LANES // rank)
    share = angles // cols
    bf16, f32 = jnp.bfloat16, jnp.float32
    dma = pltpu.SemaphoreType.DMA
    stay = pl.BlockSpec(memory_space=pltpu.HBM)
    ranks, picks = (jnp.swapaxes(x, 2, 3) for x in (coupling_rank, link_tiles))
    summed = pl.pallas_call(
        functools.partial(kernel, (doms, rows, cols)),
        out_shape=jax.ShapeDtypeStruct((share, window * tile_len), f32),
        in_specs=[stay] * 8,
        out_specs=pl.BlockSpec(memory_space=pltpu.VMEM),
        scratch_shapes=[
            pltpu.SMEM(self_rank.shape, jnp.int32),
            pltpu.SMEM(ranks.shape, jnp.int32),
            pltpu.SMEM(picks.shape, jnp.int32),
            pltpu.VMEM((rows, angles, width), bf16),
            pltpu.VMEM((rank, width), bf16),
            pltpu.VMEM((window, tiles, rank, tile_len), bf16),
            pltpu.VMEM((window, tiles, rank, tile_len), bf16),
            pltpu.VMEM((window, doms, links, rank, tile_len), bf16),
            pltpu.VMEM((doms, rows, own_tiles, angles // fold, fold * rank), bf16),
            pltpu.VMEM((window, angles, tile_len), f32),
            pltpu.VMEM((window, angles, tile_len), f32),
            pltpu.VMEM((cols - 1, window, share, tile_len), f32),
            dma((8,)),
            dma((rows - 1,)),
            dma((rows - 1,)),
            dma((doms,)),
            dma((doms,)),
            dma((doms, rows - 1)),
            dma((doms, rows - 1)),
            dma((cols - 1, window)),
            dma((cols - 1, window)),
            dma((doms, rows - 1)),
            pltpu.SemaphoreType.REGULAR,
        ]
        + [pltpu.VMEM((rows * own_tiles, angles // fold, fold * rank), bf16)] * doms,
        compiler_params=pltpu.CompilerParams(collective_id=0, has_side_effects=True, vmem_limit_bytes=16 << 20),
    )(*(pltpu.with_memory_space_constraint(x, pltpu.HBM) for x in (self_rank, ranks, picks, currents, shared_basis, self_v, self_u, coupling_u)))
    return (incident[0] - summed)[None]


def solution(mesh):
    return jax.shard_map(
        shards,
        mesh=mesh,
        in_specs=(
            P("dom", None, ("col", "row")),
            P("dom", None, "col"),
            P("dom", "row", "col", None, None),
            P("dom", "row", "col", None, None),
            P("dom", "row", "col"),
            P("dom", "row", None, "col", None, None),
            P("dom", "row", None, "col"),
            P("dom", "row", None, "col"),
            P("dom", "col", "row"),
        ),
        out_specs=P("dom", "col", "row"),
        check_vma=False,
    )
```
